32 devices in a mesh: groups: 2 (over y), segment: 4 (over z), inner: 4 (over x, core).
Axes of the slice: x: 2, y: 2, z: 4, core: 2. Of those that a mesh axis runs over, the one named last changes fastest.
Arguments:
- tokens: int32 [3, 64], P(None, 'groups'), parts along dimension 1, may hold values from 0 to 511
- embedding: bfloat16 [512, 4096], P(None, 'inner'), may hold values from -6 to 6
- in_proj: bfloat16 [4, 3, 4096, 4096], P('segment', None, None, 'inner'), may hold values from -0.09375 to 0.09375
- out_proj: bfloat16 [4, 4096, 4096], P('segment', 'inner'), may hold values from -0.09375 to 0.09375
- norm_gain: float32 [4, 4096], P('segment'), may hold values from 0.1 to 1.9
- fir_taps: float32 [4, 7, 4096], P('segment', None, 'inner'), may hold values from -2 to 2
- modal_rate: float32 [4, 8, 4096], P('segment', None, 'inner'), may hold values from 0.05 to 3
- modal_residue: float32 [4, 8, 4096], P('segment', None, 'inner'), may hold values from -2 to 2
- fir_state: float32 [4, 64, 6, 4096], P('segment', 'groups', None, 'inner'), parts along dimension 1, may hold values from -6 to 6
- modal_state: float32 [4, 64, 8, 4096], P('segment', 'groups', None, 'inner'), parts along dimension 1, may hold values from -6 to 6
- final_gain: float32 [4096], replicated, may hold values from 0.1 to 1.9
- unembed: bfloat16 [4096, 512], P(None, 'inner'), may hold values from -0.25 to 0.25
Outputs:
- logits: float32 [2, 64, 512], P(None, ('groups', 'segment'), 'inner'), parts along dimension 1
- logprob: float32 [2, 64], P(None, ('groups', 'segment')), parts along dimension 1
- fir_state_out: float32 [4, 64, 6, 4096], P('segment', 'groups', None, 'inner'), parts along dimension 1
- modal_state_out: float32 [4, 64, 8, 4096], P('segment', 'groups', None, 'inner'), parts along dimension 1
The draws below stay inside these ranges and needn't reach their ends.
There are 2 independent parts, one for each index of `groups`. The reference program is written for one: setup_inputs(seed, part) draws one part's arguments, and reference() takes and returns one part's arrays. A program takes and returns all parts, laid end to end along the dimension named above; an argument that names none is the same for every part. Nothing has to cross between parts.
All inputs are finite; a program needn't handle non-finite values.
Results may differ from the reference program's by a relative error of at most 0.025.
Values may be sent and summed in bfloat16 or wider, within the bound.
No kernel may reach another device: no remote copies, remote signals or barrier semaphores. Data moves between devices by JAX's collectives and lax.ppermute only.
A program may use at most 128 MiB of HBM per device.

```python
import math
import jax
import jax.numpy as jnp
from jax import lax

D = 4096
VOCAB = 512
R = 8
TAPS = 7
STEPS = 2
SEQS = 32
N_SEGMENT = 4


def touch_ends(result, stream_key, least, top_value):
    longest = result.shape.index(max(result.shape))
    spots = []
    for shift in (0, 1):
        where = [jax.random.randint(jax.random.fold_in(stream_key, axis), (), 0, length) for axis, length in enumerate(result.shape)]
        where[longest] = (where[longest] + shift) % result.shape[longest]
        spots.append(tuple(where))
    return result.at[spots[0]].set(least).at[spots[1]].set(top_value)


def block_levels(own_key, dims, pieces, smallest, top_value):
    def one(position, parts):
        heights = jax.random.uniform(jax.random.fold_in(jax.random.fold_in(own_key, 6), position), (parts,), jnp.float32, smallest / len(pieces), top_value / len(pieces))
        return jnp.repeat(jnp.exp(heights), dims[position] // parts).reshape((-1,) + (1,) * (len(dims) - position - 1))

    loudness = one(*pieces[0])
    for cut in pieces[1:]:
        loudness = loudness * one(*cut)
    return loudness


def bell_draw(key, extent, width, reach, cuts=(), held_as=jnp.bfloat16):
    drawn = width * jax.random.normal(key, extent, jnp.float32)
    if cuts:
        drawn = drawn * block_levels(key, extent, cuts, -0.22, 0.18)
    return jnp.clip(drawn, -reach, reach).astype(held_as)


def setup_inputs(seed: int = 0, part: int = 0) -> dict:
    key_list = jax.random.split(jax.random.key(seed), 13)
    part_splits = jax.random.split(jax.random.fold_in(key_list[12], part), 13)
    tokens = touch_ends(jax.random.randint(part_splits[0], (STEPS + 1, SEQS), 0, VOCAB), jax.random.fold_in(part_splits[0], 1), 0, VOCAB - 1).astype(jnp.int32)
    embedding = bell_draw(key_list[1], (VOCAB, D), 1.0, 6.0, ((1, 4),))
    in_proj = bell_draw(key_list[2], (N_SEGMENT, 3, D, D), D ** -0.5, 0.09375, ((0, 4), (3, 4)))
    out_proj = bell_draw(key_list[3], (N_SEGMENT, D, D), D ** -0.5, 0.09375, ((0, 4), (1, 4)))
    norm_gain = jnp.clip(1.0 + 0.18 * jax.random.normal(key_list[4], (N_SEGMENT, D), jnp.float32), 0.1, 1.9)
    fir_taps = bell_draw(key_list[5], (N_SEGMENT, TAPS, D), TAPS ** -0.5, 2.0, ((0, 4), (2, 4)), jnp.float32)
    modal_rate = jnp.clip(jnp.exp(math.log(3.0) - 4.0943445 * jax.random.uniform(key_list[6], (N_SEGMENT, R, D), jnp.float32) ** block_levels(key_list[6], (N_SEGMENT, R, D), ((0, 4), (2, 4)), -0.2, 0.2)), 0.05, 3.0)
    modal_residue = bell_draw(key_list[7], (N_SEGMENT, R, D), R ** -0.5, 2.0, ((0, 4), (2, 4)), jnp.float32)
    fir_state = bell_draw(part_splits[8], (N_SEGMENT, SEQS, TAPS - 1, D), 1.0, 6.0, ((0, 4), (3, 4)), jnp.float32)
    modal_state = bell_draw(part_splits[9], (N_SEGMENT, SEQS, R, D), 1.0, 6.0, ((0, 4), (3, 4)), jnp.float32)
    final_gain = jnp.clip(1.0 + 0.18 * jax.random.normal(key_list[10], (D,), jnp.float32), 0.1, 1.9)
    unembed = bell_draw(key_list[11], (D, VOCAB), (D // 9) ** -0.5, 0.25, ((1, 4),))
    return dict(tokens=tokens, embedding=embedding, in_proj=in_proj, out_proj=out_proj, norm_gain=norm_gain, fir_taps=fir_taps, modal_rate=modal_rate, modal_residue=modal_residue, fir_state=fir_state, modal_state=modal_state, final_gain=final_gain, unembed=unembed)


def normed(values, scale_gain):
    mean_square = lax.optimization_barrier(jnp.mean(values * values, axis=-1, keepdims=True))
    return values * lax.rsqrt(mean_square + 1e-05) * scale_gain

def reference(tokens, embedding, in_proj, out_proj, norm_gain, fir_taps, modal_rate, modal_residue, fir_state, modal_state, final_gain, unembed):
    fir_list = [fir_state[layer_index] for layer_index in range(N_SEGMENT)]
    modal_list = [modal_state[layer_index] for layer_index in range(N_SEGMENT)]
    finals = []
    for step_index in range(STEPS):
        stream = jnp.take(embedding, tokens[step_index], axis=0)
        for layer_index in range(N_SEGMENT):
            normalized = normed(stream.astype(jnp.float32), norm_gain[layer_index]).astype(jnp.bfloat16)
            projected = jnp.einsum('bd,jdc->jbc', normalized.astype(jnp.float32), in_proj[layer_index].astype(jnp.float32))
            query_part = projected[0]
            product = projected[1] * projected[2]
            taps_now = fir_taps[layer_index]
            if layer_index % 2 == 0:
                window = jnp.concatenate([fir_list[layer_index], product[:, None, :]], axis=1)
                filtered = lax.optimization_barrier(jnp.sum(window * taps_now[::-1][None], axis=1))
                fir_list[layer_index] = window[:, 1:]
            else:
                decay_factor = jnp.exp(-modal_rate[layer_index])
                mode_values = decay_factor[None] * modal_list[layer_index] + (1.0 - decay_factor[None]) * product[:, None, :]
                filtered = lax.optimization_barrier(jnp.sum(modal_residue[layer_index][None] * mode_values, axis=1)) + taps_now[0][None] * product
                modal_list[layer_index] = mode_values
            gated_rows = (query_part * filtered).astype(jnp.bfloat16)
            mixed_sum = jnp.dot(gated_rows, out_proj[layer_index], preferred_element_type=jnp.float32)
            stream = (stream.astype(jnp.float32) + mixed_sum).astype(jnp.bfloat16)
        finals.append(stream)
    final_stream = jnp.stack(finals)
    head_in = normed(final_stream.astype(jnp.float32), final_gain).astype(jnp.bfloat16)
    logits = jnp.einsum('tsd,dv->tsv', head_in.astype(jnp.float32), unembed.astype(jnp.float32))
    log_total = jnp.log(lax.optimization_barrier(jnp.sum(jnp.exp(logits), axis=-1)))
    target = jnp.take_along_axis(logits, tokens[1:][..., None], axis=-1)[..., 0]
    return (logits, target - log_total, jnp.stack(fir_list), jnp.stack(modal_list))
```

```python
import functools

import jax
import jax.numpy as jnp
from jax import lax
from jax.experimental import pallas as pl
from jax.experimental.pallas import tpu as pltpu
from jax.sharding import PartitionSpec as P

EPS = 1e-05
BOTH = ("segment", "inner")
VM = pl.BlockSpec(memory_space=pltpu.VMEM)


def in_kernel_memory(array):
    return pltpu.with_memory_space_constraint(array, pltpu.VMEM)


def lanes(index, width):
    return pl.ds(pl.multiple_of(index * width, width), width)


def column_tile(width):
    return min(512, width)


def dot(left, right):
    return jnp.dot(left, right, preferred_element_type=jnp.float32)


def scaled_half(half_ref, gain_ref, scaled, core, chips, width):
    total = None
    for chip in range(chips):
        values = half_ref[:, chip * width : (chip + 1) * width].astype(jnp.float32)
        part = jnp.sum(values * values, axis=-1, keepdims=True)
        total = part if total is None else total + part
        gain = gain_ref[:, lanes(2 * chip + core, width)]
        scaled[:, chip * width : (chip + 1) * width] = (values * gain).astype(jnp.bfloat16)
    return total


def half_product(scaled, w_in, part, core, columns, chips, width):
    total = None
    for chip in range(chips):
        rows = lanes(2 * chip + core, width)
        term = dot(scaled[:, chip * width : (chip + 1) * width], w_in[part, rows, columns])
        total = term if total is None else total + term
    return total


def first_kernel(stage, chips, own, gain, w_in, sums, squares, scaled):
    width = w_in.shape[2]
    tile = column_tile(width)

    @pl.when(lax.axis_index("segment") == stage)
    def _():
        core = lax.rem(lax.axis_index("inner"), 2)
        total = scaled_half(own, gain, scaled, core, chips, width)
        squares[...] = jnp.broadcast_to(total, squares.shape)
        for part in range(3):

            @pl.loop(0, width // tile)
            def _(step):
                columns = lanes(step, tile)
                sums[part, :, columns] = half_product(
                    scaled, w_in, part, core, columns, chips, width
                )


def second_kernel(
    stage,
    chips,
    steps,
    other,
    gain,
    w_in,
    sums,
    squares,
    fixed,
    factors,
    product_in,
    w_out,
    product,
    gated,
    partner,
    scaled,
):
    width = w_in.shape[2]
    tile = column_tile(width)
    seqs = other.shape[0] // steps
    features = w_in.shape[1]

    @pl.when(lax.axis_index("segment") == stage)
    def _():
        core = lax.rem(lax.axis_index("inner"), 2)
        facing = 1 - core
        total = scaled_half(other, gain, scaled, facing, chips, width)
        mean_square = (total + squares[:, :1]) / features
        scale = lax.rsqrt(mean_square + EPS)

        @pl.loop(0, width // tile)
        def _(step):
            columns = lanes(step, tile)
            query, key, value = (
                scale
                * (
                    sums[part, :, columns]
                    + half_product(scaled, w_in, part, facing, columns, chips, width)
                )
                for part in range(3)
            )
            fresh = key * value
            product[:, columns] = fresh
            for now in range(steps):
                rows = slice(now * seqs, (now + 1) * seqs)
                filtered = fixed[now, :, columns]
                for back in range(now + 1):
                    source = slice((now - back) * seqs, (now - back + 1) * seqs)
                    filtered = filtered + factors[back : back + 1, columns] * fresh[source]
                gated[rows, columns] = (query[rows] * filtered).astype(jnp.bfloat16)

        out_half(gated, w_out, partner, facing, chips)


def out_half(gated, w_out, result, core, chips):
    width = w_out.shape[1] // (2 * chips)
    tile = column_tile(width)
    for chip in range(chips):

        @pl.loop(0, width // tile)
        def _(step):
            source = pl.ds(pl.multiple_of((2 * chip + core) * width + step * tile, tile), tile)
            target = pl.ds(pl.multiple_of(chip * width + step * tile, tile), tile)
            result[:, target] = dot(gated[...], w_out[:, source]).astype(result.dtype)


def third_kernel(stage, chips, gated, w_out, result):
    @pl.when(lax.axis_index("segment") == stage)
    def _():
        core = lax.rem(lax.axis_index("inner"), 2)
        out_half(gated, w_out, result, core, chips)


def call(kernel, outs, args, scratch=(), aliases=None, flops=0, nbytes=0):
    return pl.pallas_call(
        kernel,
        out_shape=outs,
        in_specs=[VM] * len(args),
        out_specs=jax.tree.map(lambda _: VM, outs),
        scratch_shapes=scratch,
        input_output_aliases=aliases or {},
        compiler_params=pltpu.CompilerParams(vmem_limit_bytes=8 << 20),
        cost_estimate=pl.CostEstimate(flops=flops, bytes_accessed=nbytes, transcendentals=0),
    )(*args)


def head_kernel(
    chips, own, other, gain, unembed, targets, columns, logits, sums, head_in
):
    width = gain.shape[1] // (2 * chips)
    core = lax.rem(lax.axis_index("inner"), 2)
    total = jnp.zeros((own.shape[0], 1), jnp.float32)
    for half_ref in (own, other):
        values = half_ref[...].astype(jnp.float32)
        total = total + jnp.sum(values * values, axis=-1, keepdims=True)
    scale = lax.rsqrt(total / gain.shape[1] + EPS)
    for half_ref, which in ((own, core), (other, 1 - core)):
        for chip in range(chips):
            values = half_ref[:, chip * width : (chip + 1) * width].astype(jnp.float32)
            place = lanes(2 * chip + which, width)
            head_in[:, place] = (values * scale * gain[:, place]).astype(jnp.bfloat16)
    result = dot(head_in[...], unembed[...])
    logits[...] = result
    exp_local = jnp.sum(jnp.exp(result), axis=-1, keepdims=True)
    here = columns[...] == targets[...]
    target_local = jnp.sum(jnp.where(here, result, 0.0), axis=-1, keepdims=True)
    place = lax.broadcasted_iota(jnp.int32, sums.shape, 1)
    sums[...] = jnp.where(place == 0, exp_local, target_local)


def swap_cores(block):
    count = lax.axis_size("inner")
    return lax.ppermute(block, "inner", [(i, i ^ 1) for i in range(count)])


def short_parts(fir, taps, steps):
    held = fir.shape[1]
    fixed = []
    for now in range(steps):
        total = jnp.zeros(fir.shape[:1] + fir.shape[2:], jnp.float32)
        for back in range(now + 1, held + 1):
            total = total + fir[:, held - (back - now)] * taps[back]
        fixed.append(total)
    return jnp.stack(fixed), taps[:steps]


def modal_parts(modal, taps, rate, residue, steps):
    decay = jnp.exp(-rate)
    fixed, factors = [], []
    power = jnp.ones_like(decay)
    for now in range(steps):
        factor = jnp.sum(residue * power * (1.0 - decay), axis=0)
        factors.append(factor + taps[0] if now == 0 else factor)
        power = power * decay
        fixed.append(jnp.sum((residue * power)[None] * modal, axis=1))
    return jnp.stack(fixed), jnp.stack(factors)


def per_device(
    tokens,
    embedding,
    in_proj,
    out_proj,
    norm_gain,
    fir_taps,
    modal_rate,
    modal_residue,
    fir_state,
    modal_state,
    final_gain,
    unembed,
):
    segments = lax.axis_size("segment")
    count = lax.axis_size("inner")
    chips = count // 2
    segment = lax.axis_index("segment")
    inner = lax.axis_index("inner")
    steps = tokens.shape[0] - 1
    seqs = tokens.shape[1]
    rows = steps * seqs
    width = embedding.shape[1]
    half = chips * width
    features = half * 2
    w_in = in_kernel_memory(in_proj[0])
    w_out = in_kernel_memory(out_proj[0])
    is_short = segment % 2 == 0
    taps, rate, residue = fir_taps[0], modal_rate[0], modal_residue[0]
    fir, modal = fir_state[0], modal_state[0]

    short_fixed, short_factors = short_parts(fir, taps, steps)
    modal_fixed, modal_factors = modal_parts(modal, taps, rate, residue, steps)
    fixed = jnp.where(is_short, short_fixed, modal_fixed)
    factors = jnp.where(is_short, short_factors, modal_factors)

    picked = jnp.take(embedding, tokens[:steps].reshape(rows), axis=0)
    pieces = [None] * chips
    for hop in range(chips):
        route = [(i, (i + 2 * hop) % count) for i in range(count)]
        pieces[hop] = lax.ppermute(picked, "inner", route) if hop else picked
    chip_here = inner // 2
    stacked = jnp.stack(pieces)
    order = (chip_here - jnp.arange(chips)) % chips
    own = jnp.concatenate([stacked[order[c]] for c in range(chips)], axis=1)

    product = jnp.zeros((rows, width), jnp.float32)
    f32, bf16 = jnp.float32, jnp.bfloat16
    shape = jax.ShapeDtypeStruct
    for stage in range(segments):
        other = swap_cores(own)
        sums, squares = call(
            functools.partial(first_kernel, stage, chips),
            (shape((3, rows, width), f32), shape((rows, 128), f32)),
            (own, norm_gain, w_in),
            scratch=[pltpu.VMEM((rows, half), bf16)],
            flops=6 * rows * half * width,
            nbytes=6 * half * width,
        )
        product, gated, partner = call(
            functools.partial(second_kernel, stage, chips, steps),
            (shape((rows, width), f32), shape((rows, width), bf16), shape((rows, half), bf16)),
            (other, norm_gain, w_in, sums, squares, fixed, factors, product, w_out),
            scratch=[pltpu.VMEM((rows, half), bf16)],
            aliases={7: 0},
            flops=8 * rows * half * width,
            nbytes=8 * half * width,
        )
        facing = swap_cores(partner)
        mine = call(
            functools.partial(third_kernel, stage, chips),
            shape((rows, half), f32),
            (gated, w_out),
            flops=2 * rows * half * width,
            nbytes=2 * half * width,
        )
        share = own.astype(f32) * (1.0 / chips)
        chip_sum = (mine + facing.astype(f32) + share).astype(bf16)
        if stage < segments - 1:
            total = None
            for hop in range(chips):
                route = [
                    (stage * count + i, (stage + 1) * count + (i + 2 * hop) % count)
                    for i in range(count)
                ]
                term = lax.ppermute(chip_sum, BOTH, route).astype(f32)
                total = term if total is None else total + term
            own = total.astype(bf16)

    block = seqs // segments
    last = segments - 1
    by_block = chip_sum.reshape(steps, segments, block, half)
    total = None
    for hop in range(chips):
        for target in range(segments):
            part = by_block[:, target].reshape(steps * block, half)
            if hop == 0 and target == last:
                term = jnp.where(segment == last, part.astype(f32), 0.0)
            else:
                route = [
                    (last * count + i, target * count + (i + 2 * hop) % count)
                    for i in range(count)
                ]
                term = lax.ppermute(part, BOTH, route).astype(f32)
            total = term if total is None else total + term
    own = total.astype(bf16)
    other = swap_cores(own)
    vocab = unembed.shape[1]
    head_rows = steps * block
    wanted = lax.dynamic_slice(tokens, (1, segment * block), (steps, block))
    targets = jnp.broadcast_to(wanted.reshape(head_rows, 1), (head_rows, vocab))
    columns = jnp.broadcast_to(
        inner * vocab + jnp.arange(vocab, dtype=jnp.int32)[None], (head_rows, vocab)
    )
    logits, totals = call(
        functools.partial(head_kernel, chips),
        (shape((head_rows, vocab), f32), shape((head_rows, 128), f32)),
        (own, other, final_gain[None], in_kernel_memory(unembed), targets, columns),
        scratch=[pltpu.VMEM((head_rows, features), bf16)],
        flops=2 * head_rows * features * vocab,
        nbytes=2 * features * vocab,
    )
    totals = totals[:, :2]
    summed = totals
    for hop in range(1, count):
        route = [(i, i ^ hop if count & (count - 1) == 0 else (i + hop) % count) for i in range(count)]
        summed = summed + lax.ppermute(totals, "inner", route)
    logprob = summed[:, 1] - jnp.log(summed[:, 0])

    fresh = product.reshape(steps, seqs, width)
    fir_next = jnp.concatenate([fir, fresh.transpose(1, 0, 2)], axis=1)[:, steps:]
    decay = jnp.exp(-rate)[None]
    modal_next = modal
    for now in range(steps):
        modal_next = decay * modal_next + (1.0 - decay) * fresh[now][:, None]
    fir_out = jnp.where(is_short, fir_next, fir)
    modal_out = jnp.where(is_short, modal, modal_next)
    return (
        logits.reshape(steps, block, vocab),
        logprob.reshape(steps, block),
        fir_out[None],
        modal_out[None],
    )


def solution(mesh):
    return jax.shard_map(
        per_device,
        mesh=mesh,
        in_specs=(
            P(None, "groups"),
            P(None, "inner"),
            P("segment", None, None, "inner"),
            P("segment", "inner", None),
            P("segment", None),
            P("segment", None, "inner"),
            P("segment", None, "inner"),
            P("segment", None, "inner"),
            P("segment", "groups", None, "inner"),
            P("segment", "groups", None, "inner"),
            P(),
            P(None, "inner"),
        ),
        out_specs=(
            P(None, ("groups", "segment"), "inner"),
            P(None, ("groups", "segment")),
            P("segment", "groups", None, "inner"),
            P("segment", "groups", None, "inner"),
        ),
        check_vma=False,
    )
```

```python
import functools

import jax
import jax.numpy as jnp
from jax import lax
from jax.experimental import pallas as pl
from jax.experimental.pallas import tpu as pltpu
from jax.sharding import PartitionSpec as P

EPS = 1e-05
BOTH = ("segment", "inner")
VM = pl.BlockSpec(memory_space=pltpu.VMEM)


ANY = pl.BlockSpec(memory_space=pl.ANY)


def in_kernel_memory(array):
    return pltpu.with_memory_space_constraint(array, pltpu.VMEM)


def in_main_memory(array):
    return pltpu.with_memory_space_constraint(array, pltpu.HBM)


def load_copies(source, target, semaphores):
    rows = source.shape[-2]
    count = semaphores.shape[0]
    size = rows // count
    copies = []
    for place in range(count):
        part = slice(place * size, (place + 1) * size)
        index = (slice(None),) * (len(source.shape) - 2) + (part, slice(None))
        copies.append(
            pltpu.make_async_copy(source.at[index], target.at[index], semaphores.at[place])
        )
    return copies


def lanes(index, width):
    return pl.ds(pl.multiple_of(index * width, width), width)


def column_tile(width):
    return min(512, width)


def dot(left, right):
    return jnp.dot(left, right, preferred_element_type=jnp.float32)


def take(refs, place, width):
    if len(refs) == 1:
        return refs[0][:, place * width : (place + 1) * width]
    return refs[place][...]


def chip_at(refs, place, chips):
    if len(refs) == 1:
        return place
    return lax.rem(lax.div(lax.axis_index("inner"), 2) - place + chips, chips)


def scaled_half(refs, gain_ref, scaled, core, chips, width):
    total = None
    for place in range(chips):
        values = take(refs, place, width).astype(jnp.float32)
        part = jnp.sum(values * values, axis=-1, keepdims=True)
        total = part if total is None else total + part
        gain = gain_ref[:, lanes(2 * chip_at(refs, place, chips) + core, width)]
        scaled[:, place * width : (place + 1) * width] = (values * gain).astype(jnp.bfloat16)
    return total


def half_product(refs, scaled, w_in, part, core, columns, chips, width):
    total = None
    for place in range(chips):
        rows = lanes(2 * chip_at(refs, place, chips) + core, width)
        term = dot(scaled[:, place * width : (place + 1) * width], w_in[part, rows, columns])
        total = term if total is None else total + term
    return total


def first_kernel(stage, chips, pieces, *refs):
    own, refs = refs[:pieces], refs[pieces:]
    copies = []
    if stage == 0:
        gain, w_in, w_out, sums, squares, w_held, scaled, semaphores = refs
        copies = load_copies(w_out, w_held, semaphores)
    else:
        gain, w_in, sums, squares, scaled = refs
    for copy in copies:
        copy.start()
    width = w_in.shape[2]
    tile = column_tile(width)

    @pl.when(lax.axis_index("segment") == stage)
    def _():
        core = lax.rem(lax.axis_index("inner"), 2)
        total = scaled_half(own, gain, scaled, core, chips, width)
        squares[...] = jnp.broadcast_to(total, squares.shape)
        for part in range(3):

            @pl.loop(0, width // tile)
            def _(step):
                columns = lanes(step, tile)
                sums[part, :, columns] = half_product(
                    own, scaled, w_in, part, core, columns, chips, width
                )

    for copy in copies:
        copy.wait()


def second_kernel(stage, chips, steps, pieces, *refs):
    other, refs = refs[:pieces], refs[pieces:]
    gain, w_in, sums, squares, fixed, factors, _, w_out = refs[:8]
    product, gated, partner, scaled = refs[8:]
    width = w_in.shape[2]
    tile = column_tile(width)
    seqs = gated.shape[0] // steps
    features = w_in.shape[1]

    @pl.when(lax.axis_index("segment") == stage)
    def _():
        core = lax.rem(lax.axis_index("inner"), 2)
        facing = 1 - core
        total = scaled_half(other, gain, scaled, facing, chips, width)
        mean_square = (total + squares[:, :1]) / features
        scale = lax.rsqrt(mean_square + EPS)

        @pl.loop(0, width // tile)
        def _(step):
            columns = lanes(step, tile)
            query, key, value = (
                scale
                * (
                    sums[part, :, columns]
                    + half_product(other, scaled, w_in, part, facing, columns, chips, width)
                )
                for part in range(3)
            )
            entry = key * value
            product[:, columns] = entry
            for now in range(steps):
                rows = slice(now * seqs, (now + 1) * seqs)
                filtered = fixed[now, :, columns]
                for back in range(now + 1):
                    source = slice((now - back) * seqs, (now - back + 1) * seqs)
                    filtered = filtered + factors[back : back + 1, columns] * entry[source]
                gated[rows, columns] = (query[rows] * filtered).astype(jnp.bfloat16)

        for chip in range(chips):
            out_piece(gated, w_out, partner, chip, facing, chips, None)


def out_piece(gated, w_out, result, chip, core, chips, share):
    width = w_out.shape[1] // (2 * chips)
    tile = column_tile(width)

    @pl.loop(0, width // tile)
    def _(step):
        source = pl.ds(pl.multiple_of((2 * chip + core) * width + step * tile, tile), tile)
        target = pl.ds(pl.multiple_of(chip * width + step * tile, tile), tile)
        value = dot(gated[...], w_out[:, source])
        if share is not None:
            ref, offset = share
            columns = pl.ds(pl.multiple_of(offset + step * tile, tile), tile)
            value = value + ref[:, columns].astype(jnp.float32) * (1.0 / chips)
        result[:, target] = value.astype(result.dtype)


def third_kernel(stage, chips, pieces, *refs):
    own, (gated, w_out, result) = refs[:pieces], refs[pieces:]
    width = w_out.shape[1] // (2 * chips)

    @pl.when(lax.axis_index("segment") == stage)
    def _():
        core = lax.rem(lax.axis_index("inner"), 2)
        for place in range(chips):
            share = (own[0], place * width) if pieces == 1 else (own[place], 0)
            out_piece(gated, w_out, result, chip_at(own, place, chips), core, chips, share)


def pick_kernel(tokens, embedding, picked):
    steps, seqs = tokens.shape[0] - 1, tokens.shape[1]
    places = lax.broadcasted_iota(jnp.int32, (embedding.shape[0], seqs), 0)
    for now in range(steps):
        chosen = jnp.where(places == tokens[now : now + 1, :], 1.0, 0.0).astype(jnp.bfloat16)
        rows = lax.dot_general(
            chosen, embedding[...], (((0,), (0,)), ((), ())), preferred_element_type=jnp.float32
        )
        picked[now * seqs : (now + 1) * seqs, :] = rows.astype(jnp.bfloat16)


def prepare_kernel(
    fir, modal, taps, rate, residue, w_in, fixed, factors, product, w_held, semaphores
):
    copies = load_copies(w_in, w_held, semaphores)
    for copy in copies:
        copy.start()
    steps = fixed.shape[0]
    held = fir.shape[0]
    is_short = lax.rem(lax.axis_index("segment"), 2) == 0
    product[...] = jnp.zeros_like(product)

    @pl.when(is_short)
    def _():
        for now in range(steps):
            factors[now : now + 1, :] = taps[now]
            total = None
            for place in range(now, held):
                term = fir[place] * taps[held + now - place]
                total = term if total is None else total + term
            fixed[now] = total

    @pl.when(jnp.logical_not(is_short))
    def _():
        decay = jnp.exp(-rate[...])
        power = residue[...]
        for now in range(steps):
            factor = jnp.sum(power * (1.0 - decay), axis=0, keepdims=True)
            factors[now : now + 1, :] = factor + taps[0] if now == 0 else factor
            power = power * decay
            fixed[now] = jnp.sum(modal[...] * power[None], axis=1)

    for copy in copies:
        copy.wait()


def call(kernel, outs, args, scratch=(), aliases=None, specs=None, flops=0, nbytes=0):
    return pl.pallas_call(
        kernel,
        out_shape=outs,
        in_specs=specs or [VM] * len(args),
        out_specs=jax.tree.map(lambda _: VM, outs),
        scratch_shapes=scratch,
        input_output_aliases=aliases or {},
        compiler_params=pltpu.CompilerParams(vmem_limit_bytes=4 << 20),
        cost_estimate=pl.CostEstimate(flops=flops, bytes_accessed=nbytes, transcendentals=0),
    )(*args)


def join_kernel(*refs):
    terms, result = refs[:-1], refs[-1]
    total = terms[0][...].astype(jnp.float32)
    for term in terms[1:]:
        total = total + term[...].astype(jnp.float32)
    result[...] = total.astype(result.dtype)


def spread_kernel(steps, mine, facing, *blocks):
    seqs = mine.shape[0] // steps
    size = seqs // len(blocks)
    for place, block in enumerate(blocks):
        for now in range(steps):
            rows = slice(now * seqs + place * size, now * seqs + (place + 1) * size)
            value = mine[rows, :] + facing[rows, :].astype(jnp.float32)
            block[now * size : (now + 1) * size, :] = value.astype(block.dtype)


def collect_kernel(stage, kept, *refs):
    arrived, (_, result) = refs[:-2], refs[-2:]
    here = lax.axis_index("segment")
    for place, ref in enumerate((*arrived, kept)):

        @pl.when(here == place)
        def _():
            result[...] = ref[...]


def state_kernel(product, fir, modal, rate, fir_out, modal_out, token):
    held, seqs, width = fir.shape
    steps = product.shape[0] // seqs
    is_short = lax.rem(lax.axis_index("segment"), 2) == 0
    token[...] = jnp.zeros_like(token)

    @pl.when(is_short)
    def _():
        modal_out[...] = modal[...]
        fir_out[: held - steps] = fir[steps:]
        for now in range(steps):
            fir_out[held - steps + now] = product[now * seqs : (now + 1) * seqs, :]

    @pl.when(jnp.logical_not(is_short))
    def _():
        fir_out[...] = fir[...]
        decay = jnp.exp(-rate[...])[None]
        values = modal[...]
        for now in range(steps):
            entry = product[now * seqs : (now + 1) * seqs, :]
            values = decay * values + (1.0 - decay) * entry[:, None, :]
        modal_out[...] = values


def head_kernel(chips, own, other, gain, unembed, tokens, logits, sums, head_in):
    steps, block, vocab = logits.shape
    width = gain.shape[1] // (2 * chips)
    inner = lax.axis_index("inner")
    segment = lax.axis_index("segment")
    core = lax.rem(inner, 2)
    total = jnp.zeros((own.shape[0], 1), jnp.float32)
    for half_ref in (own, other):
        values = half_ref[...].astype(jnp.float32)
        total = total + jnp.sum(values * values, axis=-1, keepdims=True)
    scale = lax.rsqrt(total / gain.shape[1] + EPS)
    for half_ref, which in ((own, core), (other, 1 - core)):
        for chip in range(chips):
            values = half_ref[:, chip * width : (chip + 1) * width].astype(jnp.float32)
            place = lanes(2 * chip + which, width)
            head_in[:, place] = (values * scale * gain[:, place]).astype(jnp.bfloat16)
    result = dot(head_in[...], unembed[...])
    row = lax.broadcasted_iota(jnp.int32, result.shape, 0)
    column = lax.broadcasted_iota(jnp.int32, result.shape, 1) + inner * vocab
    wanted = jnp.full(result.shape, -1, jnp.int32)
    for now in range(steps):
        logits[now] = result[now * block : (now + 1) * block, :]
        for place in range(block):
            wanted = jnp.where(
                row == now * block + place, tokens[now + 1, segment * block + place], wanted
            )
    exp_local = jnp.sum(jnp.exp(result), axis=-1, keepdims=True)
    chosen = jnp.where(column == wanted, result, 0.0)
    target_local = jnp.sum(chosen, axis=-1, keepdims=True)
    place = lax.broadcasted_iota(jnp.int32, sums.shape, 1)
    sums[...] = jnp.where(place == 0, exp_local, target_local)


def total_kernel(*refs):
    parts, result = refs[:-1], refs[-1]
    steps, block = result.shape
    total = parts[0][...]
    for part in parts[1:]:
        total = total + part[...]
    column = total[:, 1:2] - jnp.log(total[:, :1])
    down = lax.broadcasted_iota(jnp.int32, (block, block), 0)
    along = lax.broadcasted_iota(jnp.int32, (block, block), 1)
    for now in range(steps):
        spread = jnp.where(down == along, column[now * block : (now + 1) * block, :], 0.0)
        result[now : now + 1, :] = jnp.sum(spread, axis=0, keepdims=True)


def swap_cores(block):
    count = lax.axis_size("inner")
    return lax.ppermute(block, "inner", [(i, i ^ 1) for i in range(count)])


def hop_chips(block, hop):
    count = lax.axis_size("inner")
    return lax.ppermute(block, "inner", [(i, (i + 2 * hop) % count) for i in range(count)])


def per_device(
    tokens,
    embedding,
    in_proj,
    out_proj,
    norm_gain,
    fir_taps,
    modal_rate,
    modal_residue,
    fir_state,
    modal_state,
    final_gain,
    unembed,
):
    segments = lax.axis_size("segment")
    count = lax.axis_size("inner")
    chips = count // 2
    steps = tokens.shape[0] - 1
    seqs = tokens.shape[1]
    rows = steps * seqs
    width = embedding.shape[1]
    half = chips * width
    features = half * 2
    f32, bf16 = jnp.float32, jnp.bfloat16
    shape = jax.ShapeDtypeStruct
    w_in = in_main_memory(in_proj[0])
    w_out = in_main_memory(out_proj[0])
    taps = fir_taps.transpose(1, 0, 2)
    rate, residue = modal_rate[0], modal_residue[0]
    fir, modal = fir_state[0].transpose(1, 0, 2), modal_state[0]

    picked = call(
        pick_kernel,
        shape((rows, width), bf16),
        (tokens, embedding),
        flops=2 * rows * width * embedding.shape[0],
        nbytes=2 * width * embedding.shape[0],
    )
    own = [hop_chips(picked, hop) if hop else picked for hop in range(chips)]
    fixed, factors, product, w_in = call(
        prepare_kernel,
        (
            shape((steps, seqs, width), f32),
            shape((steps, width), f32),
            shape((rows, width), f32),
            pltpu.VMEM(w_in.shape, bf16),
        ),
        (fir, modal, taps, rate, residue, w_in),
        specs=[VM] * 5 + [ANY],
        scratch=[pltpu.SemaphoreType.DMA((8,))],
        flops=8 * seqs * width * steps,
        nbytes=64 * seqs * width,
    )

    for stage in range(segments):
        pieces = len(own)
        other = [swap_cores(piece) for piece in own]
        outs = (shape((3, rows, width), f32), shape((rows, 128), f32))
        args = (*own, norm_gain, w_in)
        scratch = [pltpu.VMEM((rows, half), bf16)]
        specs = [VM] * len(args)
        if stage == 0:
            outs += (pltpu.VMEM(w_out.shape, bf16),)
            args += (w_out,)
            specs += [ANY]
            scratch += [pltpu.SemaphoreType.DMA((4,))]
        sums, squares, *held = call(
            functools.partial(first_kernel, stage, chips, pieces),
            outs,
            args,
            specs=specs,
            scratch=scratch,
            flops=6 * rows * half * width,
            nbytes=6 * half * width,
        )
        w_out = held[0] if held else w_out
        product, gated, partner = call(
            functools.partial(second_kernel, stage, chips, steps, pieces),
            (shape((rows, width), f32), shape((rows, width), bf16), shape((rows, half), bf16)),
            (*other, norm_gain, w_in, sums, squares, fixed, factors, product, w_out),
            scratch=[pltpu.VMEM((rows, half), bf16)],
            aliases={pieces + 6: 0},
            flops=8 * rows * half * width,
            nbytes=8 * half * width,
        )
        facing = swap_cores(partner)
        mine = call(
            functools.partial(third_kernel, stage, chips, pieces),
            shape((rows, half), f32),
            (*own, gated, w_out),
            flops=2 * rows * half * width,
            nbytes=2 * half * width,
        )
        if stage < segments - 1:
            chip_sum = call(join_kernel, shape((rows, half), bf16), (mine, facing))
            terms = []
            for hop in range(chips):
                route = [
                    (stage * count + i, (stage + 1) * count + (i + 2 * hop) % count)
                    for i in range(count)
                ]
                terms.append(lax.ppermute(chip_sum, BOTH, route))
            own = [call(join_kernel, shape((rows, half), bf16), terms)]

    block = seqs // segments
    last = segments - 1
    head_rows = steps * block
    piece = shape((head_rows, half), bf16)
    blocks = call(functools.partial(spread_kernel, steps), (piece,) * segments, (mine, facing))
    arrived = [lax.ppermute(blocks[k], "segment", [(last, k)]) for k in range(last)]
    fir_out, modal_out, token = call(
        state_kernel,
        (shape(fir.shape, f32), shape(modal.shape, f32), shape((8, 128), f32)),
        (product, fir, modal, rate),
        nbytes=8 * seqs * width * 14,
    )
    part = call(
        functools.partial(collect_kernel, last), piece, (blocks[last], *arrived, token)
    )
    hops = [hop_chips(part, hop) for hop in range(1, chips)]
    own = call(join_kernel, piece, (part, *hops))
    other = swap_cores(own)
    vocab = unembed.shape[1]
    logits, totals = call(
        functools.partial(head_kernel, chips),
        (shape((steps, block, vocab), f32), shape((head_rows, 128), f32)),
        (own, other, final_gain[None], in_kernel_memory(unembed), tokens),
        specs=[VM] * 4 + [pl.BlockSpec(memory_space=pltpu.SMEM)],
        scratch=[pltpu.VMEM((head_rows, features), bf16)],
        flops=2 * head_rows * features * vocab,
        nbytes=2 * features * vocab,
    )
    parts = [totals]
    for hop in range(1, count):
        route = [(i, (i + hop) % count) for i in range(count)]
        parts.append(lax.ppermute(totals, "inner", route))
    logprob = call(total_kernel, shape((steps, block), f32), parts)
    return logits, logprob, fir_out.transpose(1, 0, 2)[None], modal_out[None]


def solution(mesh):
    return jax.shard_map(
        per_device,
        mesh=mesh,
        in_specs=(
            P(None, "groups"),
            P(None, "inner"),
            P("segment", None, None, "inner"),
            P("segment", "inner", None),
            P("segment", None),
            P("segment", None, "inner"),
            P("segment", None, "inner"),
            P("segment", None, "inner"),
            P("segment", "groups", None, "inner"),
            P("segment", "groups", None, "inner"),
            P(),
            P(None, "inner"),
        ),
        out_specs=(
            P(None, ("groups", "segment"), "inner"),
            P(None, ("groups", "segment")),
            P("segment", "groups", None, "inner"),
            P("segment", "groups", None, "inner"),
        ),
        check_vma=False,
    )
```
